768 devices in a mesh: elem: 96 (over y, z), face: 8 (over x, core).
Axes of the slice: x: 4, y: 8, z: 12, core: 2. Of those that a mesh axis runs over, the one named last changes fastest.
Arguments:
- vol_inverse: bfloat16 [3072, 320, 320], P(('elem', 'face')), may hold values from -0.3125 to 0.3125
- vol_from_trace: bfloat16 [3072, 320, 480], P(('elem', 'face')), may hold values from -0.25 to 0.25
- trace_from_vol: bfloat16 [3072, 480, 320], P(('elem', 'face')), may hold values from -0.25 to 0.25
- vol_residual: bfloat16 [3072, 320], P(('elem', 'face')), may hold values from -6 to 6
- face_ids: int32 [3072, 6], P(('elem', 'face')), may hold values from 0 to 9215, as said below
- trace_residual: float32 [9216, 80], P(('elem', 'face')), may hold values from -6 to 6
- stabilization: float32 [9216, 80], P(('elem', 'face')), may hold values from 1.5 to 4
Outputs:
- trace_update: float32 [9216, 80], P(('elem', 'face'))
- vol_update: float32 [3072, 320], P(('elem', 'face'))
The draws below stay inside these ranges and needn't reach their ends.
Inputs may be any that keep to these rules, and one draw needn't show every extreme that they name: `face_ids`: owner group g holds elements g * 32 to (g + 1) * 32 - 1 and faces g * 96 to (g + 1) * 96 - 1. Every face is named by exactly two slots, and the 6 slots of one element name different faces. The slots of group g name faces of group g, or faces 0 to 31 of group (g - 1) mod 96; faces 0 to 31 of group g are named by one slot of group g and one slot of group (g + 1) mod 96; all other faces of group g are named by two slots of group g.
All inputs are finite; a program needn't handle non-finite values.
Results may differ from the reference program's by a relative error of at most 0.007.
Values may be sent and summed in bfloat16 or wider, within the bound.
A program may use at most 32 MiB of HBM per device.

```python
import math
import jax
import jax.numpy as jnp
from jax import lax

V = 320
W = 80
SIDES = 6
SWEEPS = 5
TRACE = 480
GROUPS = 96
E_GRP = 32
IFACE = 32
F_GRP = 96
ELEMS = 3072
FACES = 9216


def group_slots(key, group_index):
    keys = jax.random.split(key, 4)
    elem_order = jax.random.permutation(keys[0], E_GRP).astype(jnp.int32)
    face_order = jax.random.permutation(keys[1], 2 * E_GRP).astype(jnp.int32)
    side_order = jax.random.permutation(keys[2], 2 * E_GRP).astype(jnp.int32)
    offset_step = jax.random.randint(keys[3], (), 1, E_GRP).astype(jnp.int32)
    places = jnp.arange(2 * E_GRP, dtype=jnp.int32)
    pair_index = places // 2
    column = places % 2
    base = group_index * F_GRP
    inner_ids = base + IFACE + face_order
    first_elem = elem_order[pair_index]
    second_elem = elem_order[(pair_index + offset_step) % E_GRP]
    lower_base = (group_index + GROUPS - 1) % GROUPS * F_GRP
    rim_ids = jnp.where(side_order < IFACE, base + side_order, lower_base + side_order - IFACE)
    table = jnp.zeros((E_GRP, SIDES), jnp.int32)
    table = table.at[first_elem, column].set(inner_ids)
    table = table.at[second_elem, column + 2].set(inner_ids)
    table = table.at[pair_index, column + 4].set(rim_ids)
    return table


def draw_face_ids(key, part):
    keys = jax.random.split(jax.random.fold_in(key, 17), GROUPS)
    tables = jax.vmap(group_slots)(keys, jnp.arange(GROUPS, dtype=jnp.int32))
    return tables.reshape(ELEMS, SIDES).astype(jnp.int32)


def levels(stream_key, extent, cuts, least, largest):
    def one(axis_at, parts):
        steps = jax.random.uniform(jax.random.fold_in(jax.random.fold_in(stream_key, 6), axis_at), (parts,), jnp.float32, least / len(cuts), largest / len(cuts))
        return jnp.repeat(jnp.exp(steps), extent[axis_at] // parts).reshape((-1,) + (1,) * (len(extent) - axis_at - 1))

    gain = one(*cuts[0])
    for cut in cuts[1:]:
        gain = gain * one(*cut)
    return gain


def scatter_about(stream_key, dims, spread, most, pieces=(), kind=jnp.bfloat16):
    entries = spread * jax.random.normal(stream_key, dims, jnp.float32)
    if pieces:
        entries = entries * levels(stream_key, dims, pieces, -0.22, 0.18)
    return jnp.clip(entries, -most, most).astype(kind)


def setup_inputs(seed: int = 0) -> dict:
    key_list = jax.random.split(jax.random.key(seed), 8)
    return {
        "vol_inverse": scatter_about(key_list[0], (ELEMS, V, V), V ** -0.5, 0.3125, ((0, 768),)),
        "vol_from_trace": scatter_about(key_list[1], (ELEMS, V, TRACE), TRACE ** -0.5, 0.25, ((0, 768),)),
        "trace_from_vol": scatter_about(key_list[2], (ELEMS, TRACE, V), (2 * V) ** -0.5, 0.25, ((0, 768),)),
        "vol_residual": scatter_about(key_list[3], (ELEMS, V), 1.0, 6.0, ((0, 768),)),
        "face_ids": draw_face_ids(jax.random.fold_in(key_list[7], 71), 0),
        "trace_residual": scatter_about(key_list[5], (FACES, W), 1.0, 6.0, ((0, 768),), jnp.float32),
        "stabilization": jnp.clip(jnp.exp(math.log(4.0) - 0.98082925 * jax.random.uniform(key_list[6], (FACES, W), jnp.float32) ** levels(key_list[6], (FACES, W), ((0, 768),), -0.2, 0.2)), 1.5, 4.0),
    }


def reference(vol_inverse, vol_from_trace, trace_from_vol, vol_residual, face_ids, trace_residual, stabilization):
    face_total, trace_width = trace_residual.shape
    elem_total = vol_inverse.shape[0]
    slot_faces = face_ids.reshape(elem_total * SIDES).astype(jnp.int32)

    def first_pass(blocks):
        inverse, from_vol, residual = blocks
        local_row = jnp.dot(inverse, residual, preferred_element_type=jnp.float32)
        load_row = jnp.dot(from_vol, local_row.astype(jnp.bfloat16), preferred_element_type=jnp.float32)
        return local_row, load_row

    local_part, trace_load = lax.map(first_pass, (vol_inverse, trace_from_vol, vol_residual))

    def assemble(terms):
        return jax.ops.segment_sum(terms.reshape(elem_total * SIDES, trace_width), slot_faces, num_segments=face_total)

    def to_slots(trace_rows):
        return trace_rows.astype(jnp.bfloat16)[slot_faces].reshape(elem_total, SIDES * trace_width)

    right_side = trace_residual - assemble(trace_load)
    trace_now = right_side / stabilization

    def image_pass(blocks):
        inverse, up_block, from_vol, lam_row = blocks
        couple = jnp.dot(inverse, up_block, preferred_element_type=jnp.float32).astype(jnp.bfloat16)
        schur_block = jnp.dot(from_vol, couple, preferred_element_type=jnp.float32).astype(jnp.bfloat16)
        return jnp.dot(schur_block, lam_row, preferred_element_type=jnp.float32)

    for sweep_index in range(SWEEPS - 1):
        lam_elem = to_slots(trace_now)
        image_terms = lax.map(image_pass, (vol_inverse, vol_from_trace, trace_from_vol, lam_elem))
        trace_now = (right_side + assemble(image_terms)) / stabilization

    lam_elem = to_slots(trace_now)

    def back_pass(blocks):
        inverse, up_block, local_row, lam_row = blocks
        couple = jnp.dot(inverse, up_block, preferred_element_type=jnp.float32).astype(jnp.bfloat16)
        return local_row - jnp.dot(couple, lam_row, preferred_element_type=jnp.float32)

    vol_update = lax.map(back_pass, (vol_inverse, vol_from_trace, local_part, lam_elem))
    return trace_now, vol_update
```

```python
import functools

import jax
import jax.numpy as jnp
from jax import lax
from jax.experimental import pallas as pl
from jax.experimental.pallas import tpu as pltpu
from jax.sharding import PartitionSpec as P

MESH = pl.DeviceIdType.MESH
F32, BF16, I32 = jnp.float32, jnp.bfloat16, jnp.int32
SWEEPS = 5
ROWS, PARTS, SLOTS, OWN = 16, 5, 24, 12
TURNS = (4, 3, 5, 2, 6, 1, 7)
PEERS = tuple((1, i) for i in TURNS + (0,)) + tuple((-1, i) for i in TURNS + (0,)) + tuple((0, i) for i in TURNS)
SELF = len(PEERS)
KINDS = SELF + 1


def kernel(groups, members, ids, inv_hbm, up_hbm, down_hbm, vol_res, res_ref, stab_ref, trace_out, vol_out,
           inv, up, down, couple, schur, rhs_mat, first, tiles, pick, face_pick, kind_row, square,
           load_sem, send_sem, recv_sem):
    group, member = lax.axis_index("elem"), lax.axis_index("face")
    group_faces = OWN * members

    def device(shift, turn):
        return (lax.rem(group + shift + groups, groups), lax.rem(member + turn + members, members))

    loads = [
        pltpu.make_async_copy(src, dst, load_sem.at[n])
        for n, (src, dst) in enumerate(((inv_hbm, inv), (down_hbm, down), (up_hbm, up)))
    ]
    for copy in loads:
        copy.start()
    barrier = pltpu.get_barrier_semaphore()
    for shift, turn in PEERS:
        pl.semaphore_signal(barrier, inc=1, device_id=device(shift, turn), device_id_type=MESH)

    lane = lax.broadcasted_iota(I32, (1, 256), 1)

    def steps(x, width, count):
        return sum((x >= width * n).astype(I32) for n in range(1, count))

    half = lane >= 128
    inner = jnp.where(half, lax.bitwise_and(lane, 63), lane)
    part = jnp.where(half, steps(inner, OWN, PARTS), steps(inner, SLOTS, PARTS))
    index = inner - part * jnp.where(half, OWN, SLOTS)
    used = inner < jnp.where(half, OWN * PARTS, SLOTS * PARTS)
    own_base = group * group_faces + member * OWN
    wanted = own_base + index
    for s in range(SLOTS):
        wanted = jnp.where(jnp.logical_and(lane < 128, index == s), ids[s % 4, s // 4], wanted)
    wanted = jnp.where(used, wanted, -1)
    wanted_f = wanted.astype(F32)

    square[...] = jnp.zeros_like(square)
    square[0:OWN, 0:80] = res_ref[...]
    square[64 : 64 + OWN, 0:80] = stab_ref[...]
    turned = square[...].T
    small = lax.broadcasted_iota(I32, (ROWS, 128), 1)
    low = lax.bitwise_and(small, 63)
    faces = jnp.zeros((ROWS, 128), F32)
    for j in range(PARTS):
        block = turned[j * ROWS : (j + 1) * ROWS]
        block = pltpu.roll(block, j * OWN, 1) if j else block
        faces = jnp.where(jnp.logical_and(low >= j * OWN, low < (j + 1) * OWN), block, faces)
    first[SELF, 0:ROWS] = faces
    first[SELF, ROWS : ROWS + 8] = jnp.broadcast_to(wanted_f[:, :128], (8, 128))

    def send(phase, ref):
        for n, (shift, turn) in enumerate(PEERS):
            pltpu.make_async_remote_copy(
                src_ref=ref.at[SELF],
                dst_ref=ref.at[n],
                send_sem=send_sem.at[phase],
                recv_sem=recv_sem.at[phase],
                device_id=device(shift, turn),
                device_id_type=MESH,
            ).start()

    def arrive(phase, ref, sem):
        some = ref.at[pl.ds(0, SELF)]
        pltpu.make_async_copy(some, some, sem.at[phase]).wait()

    pl.semaphore_wait(barrier, SELF)
    send(0, first)

    def merged(products):
        total = products[0]
        for e in range(1, 4):
            at = lax.broadcasted_iota(I32, total.shape, 1)
            total = jnp.where(at == e, products[e], total)
        return total

    def to_tile(column):
        tile = jnp.zeros((ROWS, 128), F32)
        for j in range(PARTS):
            for k in range(6):
                begin = k * 80 + j * ROWS
                place = j * SLOTS + k * 4
                block = column[begin : begin + ROWS]
                block = pltpu.roll(block, place, 1) if place else block
                tile = jnp.where(jnp.logical_and(small >= place, small < place + 4), block, tile)
        return tile

    loads[0].wait()
    res_rows = jnp.concatenate([vol_res[...], jnp.zeros((124, 320), BF16)], axis=0)
    across = (((1,), (1,)), ((), ()))
    local = merged([
        lax.dot_general(inv[e], res_rows, across, preferred_element_type=F32) for e in range(4)
    ])
    local_half = local.astype(BF16)
    loads[1].wait()
    own = to_tile(merged([jnp.dot(down[e], local_half, preferred_element_type=F32) for e in range(4)]))
    tiles[0, SELF] = own.astype(BF16)
    send(1, tiles.at[0])

    loads[2].wait()
    rhs_mat[480:512] = jnp.zeros((32, 128), BF16)

    def condense(e, carry):
        block = jnp.dot(inv[e], up[e], preferred_element_type=F32).astype(BF16)
        block = jnp.concatenate([block, jnp.zeros((320, 32), BF16)], axis=1)
        couple[e] = block
        schur[e] = jnp.dot(down[e], block, preferred_element_type=F32).astype(BF16)
        return carry

    lax.fori_loop(0, 4, condense, 0)

    arrive(0, first, recv_sem)
    eight = lax.broadcasted_iota(I32, (8, 128), 0)
    for base in range(0, KINDS, 8):
        rows = jnp.zeros((8, 128), F32)
        for n in range(8):
            rows = jnp.where(eight == n, first[base + n, ROWS : ROWS + 8], rows)
        square[base : base + 8] = rows
    square[KINDS:32] = jnp.zeros((32 - KINDS, 128), F32)
    held = square[...].T
    slot_row = lax.broadcasted_iota(I32, (SLOTS, 256), 0)
    wide = jnp.broadcast_to(wanted_f, (SLOTS, 256))
    total = jnp.zeros((SLOTS, 256), F32)
    least = jnp.full((SLOTS, 256), 4096.0, F32)
    for n in range(KINDS):
        hit = jnp.broadcast_to(held[0:SLOTS, n : n + 1], (SLOTS, 256)) == wide
        code = (slot_row + 32 * n).astype(F32)
        total = total + jnp.where(hit, code, 0.0)
        least = jnp.minimum(least, jnp.where(hit, code, 4096.0))
    total = jnp.sum(total, axis=0, keepdims=True)
    least = jnp.min(least, axis=0, keepdims=True)
    self_code = (SELF * 32 + index).astype(F32)
    code = jnp.where(half, jnp.where(lane < 192, least, total - least), total - self_code)
    code = code.astype(I32)
    kinds = jnp.where(used, lax.shift_right_arithmetic(code, 5), -1)
    row = part * SLOTS + lax.bitwise_and(code, 31)
    deep = lax.broadcasted_iota(I32, (128, 256), 0)
    pick[...] = jnp.where(jnp.logical_and(deep == row, used), 1.0, 0.0).astype(BF16)
    kind_row[...] = jnp.broadcast_to(kinds, (ROWS, 256))

    owner = jnp.full((1, 128), -1, I32)
    place = jnp.zeros((1, 128), I32)
    sources = [n for n in range(SELF) if PEERS[n][0] >= 0] + [SELF]
    for n in sources:
        shift, turn = PEERS[n] if n < SELF else (0, 0)
        base = lax.rem(group - shift + groups, groups) * group_faces + lax.rem(member - turn + members, members) * OWN
        offset = wanted[:, :128] - base
        hit = jnp.logical_and(offset >= 0, offset < OWN)
        owner = jnp.where(hit, n, owner)
        place = jnp.where(hit, offset, place)
    place = part[:, :128] * OWN + place
    slim = lax.broadcasted_iota(I32, (128, 128), 0)
    face_pick[:, 0:128] = jnp.where(slim == place, 1.0, 0.0)
    face_pick[:, 128:256] = jnp.where(slim == place + 64, 1.0, 0.0)
    sent = jnp.concatenate([first[n, 0:ROWS] for n in sources], axis=0)
    found = jnp.dot(sent, face_pick[...], preferred_element_type=F32, precision=lax.Precision.HIGHEST)
    owner_rows = jnp.broadcast_to(owner, (ROWS, 128))
    right = jnp.zeros((ROWS, 128), F32)
    stab = jnp.zeros((ROWS, 128), F32)
    for at, n in enumerate(sources):
        block = found[at * ROWS : (at + 1) * ROWS]
        right = jnp.where(owner_rows == n, block[:, :128], right)
        stab = jnp.where(owner_rows == n, block[:, 128:], stab)
    scale = 1.0 / jnp.where(owner_rows >= 0, stab, 1.0)
    face_stab = pltpu.roll(first[SELF, 0:ROWS], 64, 1)
    face_scale = 1.0 / jnp.where(small < OWN * PARTS, face_stab, 1.0)

    def gathered(phase, width):
        stack = tiles[phase].reshape(KINDS * ROWS, 128)
        found = jnp.dot(stack, pick[:, 0:width], preferred_element_type=F32)
        kinds = kind_row[:, 0:width]
        total = jnp.zeros((ROWS, width), F32)
        for n in range(KINDS):
            total = jnp.where(kinds == n, found[n * ROWS : (n + 1) * ROWS], total)
        return total

    def face_sum(both):
        return both[:, 128:] + pltpu.roll(both[:, 128:], 64, 1)

    def spread(lam):
        for k in range(6):
            for j in range(PARTS):
                place = j * SLOTS + k * 4
                block = pltpu.roll(lam, 128 - place, 1) if place else lam
                rhs_mat[k * 80 + j * ROWS : k * 80 + (j + 1) * ROWS] = block.astype(BF16)

    arrive(1, tiles.at[0], recv_sem)
    both = gathered(0, 256)
    right = right - (own + both[:, :128])
    face_right = first[SELF, 0:ROWS] - face_sum(both)
    spread(right * scale)
    for sweep in range(1, SWEEPS):
        own = to_tile(merged([
            jnp.dot(schur[e], rhs_mat[...], preferred_element_type=F32) for e in range(4)
        ]))
        tiles[sweep, SELF] = own.astype(BF16)
        send(sweep + 1, tiles.at[sweep])
        arrive(sweep + 1, tiles.at[sweep], recv_sem)
        both = gathered(sweep, 256 if sweep == SWEEPS - 1 else 128)
        spread((right + own + both[:, :128]) * scale)

    face_now = (face_right + face_sum(both)) * face_scale
    for j in range(PARTS):
        block = pltpu.roll(face_now, 128 - j * OWN, 1) if j else face_now
        square[j * ROWS : (j + 1) * ROWS] = block
    trace_out[...] = square[...].T[0:OWN, 0:80]
    back = merged([jnp.dot(couple[e], rhs_mat[...], preferred_element_type=F32) for e in range(4)])
    answer = jnp.concatenate([local - back, jnp.zeros((64, 128), F32)], axis=0)
    for n in range(3):
        width = min(128, 320 - n * 128)
        vol_out[:, n * 128 : n * 128 + width] = answer[n * 128 : (n + 1) * 128].T[0:4, 0:width]

    arrive(0, first, send_sem)
    for phase in range(SWEEPS):
        arrive(phase + 1, tiles.at[phase], send_sem)


def solution(mesh):
    groups, members = mesh.shape["elem"], mesh.shape["face"]
    spec2, spec3 = P(("elem", "face"), None), P(("elem", "face"), None, None)

    def local(vol_inverse, vol_from_trace, trace_from_vol, vol_residual, face_ids, trace_residual, stabilization):
        vmem, hbm = pl.BlockSpec(memory_space=pltpu.VMEM), pl.BlockSpec(memory_space=pl.ANY)
        return pl.pallas_call(
            functools.partial(kernel, groups, members),
            out_shape=(
                jax.ShapeDtypeStruct(trace_residual.shape, F32),
                jax.ShapeDtypeStruct(vol_residual.shape, F32),
            ),
            in_specs=[pl.BlockSpec(memory_space=pltpu.SMEM), hbm, hbm, hbm, vmem, vmem, vmem],
            out_specs=(vmem, vmem),
            scratch_shapes=[
                pltpu.VMEM((4, 320, 320), BF16),
                pltpu.VMEM((4, 320, 480), BF16),
                pltpu.VMEM((4, 480, 320), BF16),
                pltpu.VMEM((4, 320, 512), BF16),
                pltpu.VMEM((4, 480, 512), BF16),
                pltpu.VMEM((512, 128), BF16),
                pltpu.VMEM((KINDS, ROWS + 8, 128), F32),
                pltpu.VMEM((SWEEPS, KINDS, ROWS, 128), BF16),
                pltpu.VMEM((128, 256), BF16),
                pltpu.VMEM((128, 256), F32),
                pltpu.VMEM((ROWS, 256), I32),
                pltpu.VMEM((128, 128), F32),
                pltpu.SemaphoreType.DMA((3,)),
                pltpu.SemaphoreType.DMA((SWEEPS + 1,)),
                pltpu.SemaphoreType.DMA((SWEEPS + 1,)),
            ],
            compiler_params=pltpu.CompilerParams(collective_id=0, has_side_effects=True),
            name="newton",
        )(face_ids, vol_inverse, vol_from_trace, trace_from_vol, vol_residual, trace_residual, stabilization)

    return jax.shard_map(
        local,
        mesh=mesh,
        in_specs=(spec3, spec3, spec3, spec2, spec2, spec2, spec2),
        out_specs=(spec2, spec2),
        check_vma=False,
    )
```

```python
import functools

import jax
import jax.numpy as jnp
from jax import lax
from jax.experimental import pallas as pl
from jax.experimental.pallas import tpu as pltpu
from jax.sharding import PartitionSpec as P

MESH = pl.DeviceIdType.MESH
F32, BF16, I32 = jnp.float32, jnp.bfloat16, jnp.int32
SWEEPS = 5
ROWS, PARTS, SLOTS, OWN = 16, 5, 24, 12
TURNS = (4, 3, 5, 2, 6, 1, 7)
PEERS = tuple((1, i) for i in TURNS + (0,)) + tuple((-1, i) for i in TURNS + (0,)) + tuple((0, i) for i in TURNS)
SELF = len(PEERS)
KINDS = SELF + 1


def kernel(groups, members, ids_hbm, inv_hbm, up_hbm, down_hbm, vol_hbm, res_hbm, stab_hbm, trace_out, vol_out,
           ids, vol_res, res_ref, stab_ref, inv, up, down, couple, schur, rhs_mat, first, tiles, pick, face_pick,
           kind_row, square, load_sem, send_sem, recv_sem):
    group, member = lax.axis_index("elem"), lax.axis_index("face")
    group_faces = OWN * members

    def device(shift, turn):
        return (lax.rem(group + shift + groups, groups), lax.rem(member + turn + members, members))

    barrier = pltpu.get_barrier_semaphore()
    for shift, turn in PEERS:
        pl.semaphore_signal(barrier, inc=1, device_id=device(shift, turn), device_id_type=MESH)
    pairs = ((vol_hbm, vol_res), (inv_hbm, inv), (down_hbm, down), (ids_hbm, ids), (res_hbm, res_ref),
             (stab_hbm, stab_ref), (up_hbm, up))
    loads = [pltpu.make_async_copy(src, dst, load_sem.at[n]) for n, (src, dst) in enumerate(pairs)]
    for copy in loads:
        copy.start()

    lane = lax.broadcasted_iota(I32, (1, 256), 1)

    def steps(x, width, count):
        return sum((x >= width * n).astype(I32) for n in range(1, count))

    half = lane >= 128
    inner = jnp.where(half, lax.bitwise_and(lane, 63), lane)
    part = jnp.where(half, steps(inner, OWN, PARTS), steps(inner, SLOTS, PARTS))
    index = inner - part * jnp.where(half, OWN, SLOTS)
    used = inner < jnp.where(half, OWN * PARTS, SLOTS * PARTS)
    small = lax.broadcasted_iota(I32, (ROWS, 128), 1)
    low = lax.bitwise_and(small, 63)
    fourth = lax.bitwise_and(small, 3)
    for e in range(4):
        rhs_mat[e * 512 + 480 : (e + 1) * 512] = jnp.zeros((32, 128), BF16)

    def send(phase, ref):
        for n, (shift, turn) in enumerate(PEERS):
            pltpu.make_async_remote_copy(
                src_ref=ref.at[SELF],
                dst_ref=ref.at[n],
                send_sem=send_sem.at[phase],
                recv_sem=recv_sem.at[phase],
                device_id=device(shift, turn),
                device_id_type=MESH,
            ).start()

    def arrive(phase, ref, sem):
        some = ref.at[pl.ds(0, SELF)]
        pltpu.make_async_copy(some, some, sem.at[phase]).wait()

    loads[3].wait()
    own_base = group * group_faces + member * OWN
    wanted = own_base + index
    for s in range(SLOTS):
        wanted = jnp.where(jnp.logical_and(lane < 128, index == s), ids[s % 4, s // 4], wanted)
    wanted = jnp.where(used, wanted, -1)
    wanted_f = wanted.astype(F32)
    square[...] = jnp.zeros_like(square)
    loads[4].wait()
    square[0:OWN, 0:80] = res_ref[...]
    loads[5].wait()
    square[64 : 64 + OWN, 0:80] = stab_ref[...]
    turned = square[...].T
    faces = jnp.zeros((ROWS, 128), F32)
    for j in range(PARTS):
        block = turned[j * ROWS : (j + 1) * ROWS]
        block = pltpu.roll(block, j * OWN, 1) if j else block
        faces = jnp.where(jnp.logical_and(low >= j * OWN, low < (j + 1) * OWN), block, faces)
    first[SELF, 0:ROWS] = faces
    first[SELF, ROWS : ROWS + 8] = jnp.broadcast_to(wanted_f[:, :128], (8, 128))

    loads[0].wait()
    res_rows = jnp.concatenate([vol_res[...], jnp.zeros((124, 320), BF16)], axis=0)
    across = (((1,), (1,)), ((), ()))
    loads[1].wait()
    local = lax.dot_general(inv[0], res_rows, across, preferred_element_type=F32)
    at = lax.broadcasted_iota(I32, local.shape, 1)
    for e in range(1, 4):
        local = jnp.where(at == e, lax.dot_general(inv[e], res_rows, across, preferred_element_type=F32), local)
    local = jnp.concatenate([local, jnp.zeros((64, 128), F32)], axis=0)
    local = jnp.concatenate([local[n * 128 : (n + 1) * 128].T[0:ROWS] for n in range(3)], axis=1)
    local_rows = local[0:8]
    level = lax.broadcasted_iota(I32, (ROWS, 320), 0)
    local = jnp.concatenate(
        [jnp.where(level == e, local[:, 0:320], 0.0).astype(BF16) for e in range(4)], axis=1
    )
    loads[2].wait()
    load = jnp.zeros((ROWS, 480), F32)
    for e in range(4):
        load = load + jnp.dot(local[:, e * 320 : (e + 1) * 320], down[e], preferred_element_type=F32)
    load = jnp.concatenate([load, jnp.zeros((ROWS, 32), F32)], axis=1)
    load = jnp.concatenate([load, jnp.zeros((112, 512), F32)], axis=0)
    load = jnp.concatenate([load[:, n * 128 : (n + 1) * 128].T for n in range(4)], axis=0)
    own = jnp.zeros((ROWS, 128), F32)
    for j in range(PARTS):
        for k in range(6):
            begin = k * 80 + j * ROWS
            place = j * SLOTS + k * 4
            block = load[begin : begin + ROWS]
            block = pltpu.roll(block, place, 1) if place else block
            own = jnp.where(jnp.logical_and(small >= place, small < place + 4), block, own)
    tiles[0, SELF] = own.astype(BF16)

    pl.semaphore_wait(barrier, SELF)
    send(0, first)
    send(1, tiles.at[0])

    loads[6].wait()

    def condense(e, carry):
        block = jnp.dot(inv[e], up[e], preferred_element_type=F32).astype(BF16)
        block = jnp.concatenate([block, jnp.zeros((320, 32), BF16)], axis=1)
        columns = pl.ds(pl.multiple_of(e * 512, 512), 512)
        couple[:, columns] = block
        schur[:, columns] = lax.dot_general(
            down[e], block, (((0,), (0,)), ((), ())), preferred_element_type=F32
        ).astype(BF16)
        return carry

    lax.fori_loop(0, 4, condense, 0)

    arrive(0, first, recv_sem)
    eight = lax.broadcasted_iota(I32, (8, 128), 0)
    for base in range(0, KINDS, 8):
        rows = jnp.zeros((8, 128), F32)
        for n in range(8):
            rows = jnp.where(eight == n, first[base + n, ROWS : ROWS + 8], rows)
        square[base : base + 8] = rows
    square[KINDS:32] = jnp.zeros((32 - KINDS, 128), F32)
    held = square[...].T
    slot_row = lax.broadcasted_iota(I32, (SLOTS, 128), 0).astype(F32)
    wide_slot = jnp.broadcast_to(wanted_f[:, :128], (SLOTS, 128))
    wide_face = jnp.broadcast_to(wanted_f[:, 128:], (SLOTS, 128))
    slot_sum = jnp.zeros((SLOTS, 128), F32)
    face_total = jnp.zeros((SLOTS, 128), F32)
    least = jnp.full((SLOTS, 128), 4096.0, F32)
    for n in range(KINDS):
        column = jnp.broadcast_to(held[0:SLOTS, n : n + 1], (SLOTS, 128))
        code = slot_row + 32.0 * n
        slot_sum = slot_sum + jnp.where(column == wide_slot, code, 0.0)
        if n < SELF and PEERS[n][0] > 0:
            continue
        hit = column == wide_face
        face_total = face_total + jnp.where(hit, code, 0.0)
        least = jnp.minimum(least, jnp.where(hit, code, 4096.0))
    slot_sum = jnp.sum(slot_sum, axis=0, keepdims=True) - (SELF * 32 + index[:, :128]).astype(F32)
    face_total = jnp.sum(face_total, axis=0, keepdims=True)
    least = jnp.min(least, axis=0, keepdims=True)
    face_code = jnp.where(lane[:, :128] < 64, least, face_total - least)
    code = jnp.concatenate([slot_sum, face_code], axis=1).astype(I32)
    kinds = jnp.where(used, lax.shift_right_arithmetic(code, 5), -1)
    row = jnp.where(used, part * SLOTS + lax.bitwise_and(code, 31), -1)
    deep = lax.broadcasted_iota(I32, (128, 256), 0)
    pick[...] = jnp.where(deep == row, 1.0, 0.0).astype(BF16)
    kind_row[...] = jnp.broadcast_to(kinds, (ROWS, 256))

    owner = jnp.full((1, 128), -1, I32)
    place = jnp.zeros((1, 128), I32)
    sources = [n for n in range(SELF) if PEERS[n][0] >= 0] + [SELF]
    for n in sources:
        shift, turn = PEERS[n] if n < SELF else (0, 0)
        base = lax.rem(group - shift + groups, groups) * group_faces + lax.rem(member - turn + members, members) * OWN
        offset = wanted[:, :128] - base
        hit = jnp.logical_and(offset >= 0, offset < OWN)
        owner = jnp.where(hit, n, owner)
        place = jnp.where(hit, offset, place)
    place = part[:, :128] * OWN + place
    slim = lax.broadcasted_iota(I32, (128, 128), 0)
    face_pick[:, 0:128] = jnp.where(slim == place, 1.0, 0.0)
    face_pick[:, 128:256] = jnp.where(slim == place + 64, 1.0, 0.0)
    sent = jnp.concatenate([first[n, 0:ROWS] for n in sources], axis=0)
    found = jnp.dot(sent, face_pick[...], preferred_element_type=F32, precision=lax.Precision.HIGHEST)
    owner_rows = jnp.broadcast_to(owner, (ROWS, 128))
    right = jnp.zeros((ROWS, 128), F32)
    stab = jnp.zeros((ROWS, 128), F32)
    for at, n in enumerate(sources):
        block = found[at * ROWS : (at + 1) * ROWS]
        right = jnp.where(owner_rows == n, block[:, :128], right)
        stab = jnp.where(owner_rows == n, block[:, 128:], stab)
    scale = 1.0 / jnp.where(owner_rows >= 0, stab, 1.0)
    face_stab = pltpu.roll(first[SELF, 0:ROWS], 64, 1)
    face_scale = 1.0 / jnp.where(small < OWN * PARTS, face_stab, 1.0)

    def gathered(phase, width):
        stack = tiles[phase].reshape(KINDS * ROWS, 128)
        found = jnp.dot(stack, pick[:, 0:width], preferred_element_type=F32)
        kinds = kind_row[:, 0:width]
        total = []
        for begin in range(0, KINDS, 6):
            some = jnp.zeros((ROWS, width), F32)
            for n in range(begin, begin + 6):
                some = jnp.where(kinds == n, found[n * ROWS : (n + 1) * ROWS], some)
            total.append(some)
        return (total[0] + total[1]) + (total[2] + total[3])

    def face_sum(both):
        return both[:, 128:] + pltpu.roll(both[:, 128:], 64, 1)

    ones = [jnp.where(fourth == e, 1.0, 0.0).astype(BF16) for e in range(4)]

    def spread(lam):
        for k in range(6):
            for j in range(PARTS):
                block = jnp.take_along_axis(lam, fourth + (j * SLOTS + k * 4), axis=1).astype(BF16)
                begin = k * 80 + j * ROWS
                for e in range(4):
                    rhs_mat[e * 512 + begin : e * 512 + begin + ROWS] = block * ones[e]

    def image():
        product = jnp.dot(schur[...], rhs_mat[...], preferred_element_type=F32)
        tile = []
        for j in range(PARTS):
            some = jnp.zeros((ROWS, 128), F32)
            for k in range(6):
                place, begin = j * SLOTS + k * 4, k * 80 + j * ROWS
                fits = jnp.logical_and(small >= place, small < place + 4)
                some = jnp.where(fits, product[begin : begin + ROWS], some)
            tile.append(some)
        return (tile[0] + tile[1]) + (tile[2] + tile[3]) + tile[4]

    arrive(1, tiles.at[0], recv_sem)
    both = gathered(0, 256)
    right = right - (own + both[:, :128])
    face_right = first[SELF, 0:ROWS] - face_sum(both)
    spread(right * scale)
    for sweep in range(1, SWEEPS):
        own = image()
        tiles[sweep, SELF] = own.astype(BF16)
        send(sweep + 1, tiles.at[sweep])
        arrive(sweep + 1, tiles.at[sweep], recv_sem)
        both = gathered(sweep, 256 if sweep == SWEEPS - 1 else 128)
        spread((right + own + both[:, :128]) * scale)

    face_now = (face_right + face_sum(both)) * face_scale
    for j in range(PARTS):
        block = pltpu.roll(face_now, 128 - j * OWN, 1) if j else face_now
        square[j * ROWS : (j + 1) * ROWS] = block
    trace_out[...] = square[...].T[0:ROWS]
    back = jnp.dot(couple[...], rhs_mat[...], preferred_element_type=F32)
    back = jnp.concatenate([back, jnp.zeros((64, 128), F32)], axis=0)
    for n in range(3):
        columns = slice(n * 128, (n + 1) * 128)
        vol_out[:, columns] = local_rows[:, columns] - back[columns].T[0:8]

    arrive(0, first, send_sem)
    for phase in range(SWEEPS):
        arrive(phase + 1, tiles.at[phase], send_sem)


def write(trace_in, vol_in, trace_out, vol_out):
    trace_out[...] = trace_in[0:OWN, 0:80]
    vol_out[...] = vol_in[0:4, 0:320]


def solution(mesh):
    groups, members = mesh.shape["elem"], mesh.shape["face"]
    spec2, spec3 = P(("elem", "face"), None), P(("elem", "face"), None, None)

    def local(vol_inverse, vol_from_trace, trace_from_vol, vol_residual, face_ids, trace_residual, stabilization):
        vmem, hbm = pl.BlockSpec(memory_space=pltpu.VMEM), pl.BlockSpec(memory_space=pl.ANY)
        trace, vol = pl.pallas_call(
            functools.partial(kernel, groups, members),
            out_shape=(pltpu.VMEM((ROWS, 128), F32), pltpu.VMEM((8, 384), F32)),
            in_specs=[hbm] * 7,
            out_specs=(vmem, vmem),
            scratch_shapes=[
                pltpu.SMEM((4, 6), I32),
                pltpu.VMEM((4, 320), BF16),
                pltpu.VMEM((OWN, 80), F32),
                pltpu.VMEM((OWN, 80), F32),
                pltpu.VMEM((4, 320, 320), BF16),
                pltpu.VMEM((4, 320, 480), BF16),
                pltpu.VMEM((4, 320, 480), BF16),
                pltpu.VMEM((320, 2048), BF16),
                pltpu.VMEM((480, 2048), BF16),
                pltpu.VMEM((2048, 128), BF16),
                pltpu.VMEM((KINDS, ROWS + 8, 128), F32),
                pltpu.VMEM((SWEEPS, KINDS, ROWS, 128), BF16),
                pltpu.VMEM((128, 256), BF16),
                pltpu.VMEM((128, 256), F32),
                pltpu.VMEM((ROWS, 256), I32),
                pltpu.VMEM((128, 128), F32),
                pltpu.SemaphoreType.DMA((7,)),
                pltpu.SemaphoreType.DMA((SWEEPS + 1,)),
                pltpu.SemaphoreType.DMA((SWEEPS + 1,)),
            ],
            compiler_params=pltpu.CompilerParams(collective_id=0, has_side_effects=True),
            name="newton",
        )(
            face_ids, vol_inverse, vol_from_trace, jnp.swapaxes(trace_from_vol, 1, 2), vol_residual,
            trace_residual, stabilization,
        )
        return pl.pallas_call(
            write,
            out_shape=(
                jax.ShapeDtypeStruct(trace_residual.shape, F32),
                jax.ShapeDtypeStruct(vol_residual.shape, F32),
            ),
            in_specs=[vmem, vmem],
            out_specs=(vmem, vmem),
            name="write",
        )(pltpu.with_memory_space_constraint(trace, pltpu.VMEM), pltpu.with_memory_space_constraint(vol, pltpu.VMEM))

    return jax.shard_map(
        local,
        mesh=mesh,
        in_specs=(spec3, spec3, spec3, spec2, spec2, spec2, spec2),
        out_specs=(spec2, spec2),
        check_vma=False,
    )
```

```python
import functools

import jax
import jax.numpy as jnp
from jax import lax
from jax.experimental import pallas as pl
from jax.experimental.pallas import tpu as pltpu
from jax.sharding import PartitionSpec as P

MESH = pl.DeviceIdType.MESH
F32, BF16, I32 = jnp.float32, jnp.bfloat16, jnp.int32
SWEEPS = 5
ROWS, PARTS, SLOTS, OWN = 16, 5, 24, 12
TURNS = (4, 3, 5, 2, 6, 1, 7)
PEERS = tuple((1, i) for i in TURNS + (0,)) + tuple((-1, i) for i in TURNS + (0,)) + tuple((0, i) for i in TURNS)
SELF = len(PEERS)
KINDS = SELF + 1


def kernel(groups, members, ids_hbm, inv_hbm, up_hbm, down_hbm, vol_hbm, res_hbm, stab_hbm, trace_out, vol_out,
           ids, vol_res, res_ref, stab_ref, inv, up, down, couple, schur, rhs_mat, first, tiles, pick, face_pick,
           kind_row, square, load_sem, send_sem, recv_sem):
    group, member = lax.axis_index("elem"), lax.axis_index("face")
    group_faces = OWN * members

    def device(shift, turn):
        return (lax.rem(group + shift + groups, groups), lax.rem(member + turn + members, members))

    barrier = pltpu.get_barrier_semaphore()
    for shift, turn in PEERS:
        pl.semaphore_signal(barrier, inc=1, device_id=device(shift, turn), device_id_type=MESH)
    pairs = ((vol_hbm, vol_res), (inv_hbm, inv), (down_hbm, down), (ids_hbm, ids), (res_hbm, res_ref),
             (stab_hbm, stab_ref), (up_hbm, up))
    loads = [pltpu.make_async_copy(src, dst, load_sem.at[n]) for n, (src, dst) in enumerate(pairs)]
    for copy in loads:
        copy.start()

    lane = lax.broadcasted_iota(I32, (1, 256), 1)

    def steps(x, width, count):
        return sum((x >= width * n).astype(I32) for n in range(1, count))

    half = lane >= 128
    inner = jnp.where(half, lax.bitwise_and(lane, 63), lane)
    part = jnp.where(half, steps(inner, OWN, PARTS), steps(inner, SLOTS, PARTS))
    index = inner - part * jnp.where(half, OWN, SLOTS)
    used = inner < jnp.where(half, OWN * PARTS, SLOTS * PARTS)
    small = lax.broadcasted_iota(I32, (ROWS, 128), 1)
    low = lax.bitwise_and(small, 63)
    fourth = lax.bitwise_and(small, 3)
    rhs_mat[480:512] = jnp.zeros((32, 128), BF16)
    rhs_mat[992:1024] = jnp.zeros((32, 128), BF16)

    def send(phase, ref):
        for n, (shift, turn) in enumerate(PEERS):
            pltpu.make_async_remote_copy(
                src_ref=ref.at[SELF],
                dst_ref=ref.at[n],
                send_sem=send_sem.at[phase],
                recv_sem=recv_sem.at[phase],
                device_id=device(shift, turn),
                device_id_type=MESH,
            ).start()

    def arrive(phase, ref, sem):
        some = ref.at[pl.ds(0, SELF)]
        pltpu.make_async_copy(some, some, sem.at[phase]).wait()

    loads[3].wait()
    own_base = group * group_faces + member * OWN
    wanted = own_base + index
    for s in range(SLOTS):
        wanted = jnp.where(jnp.logical_and(lane < 128, index == s), ids[s % 4, s // 4], wanted)
    wanted = jnp.where(used, wanted, -1)
    wanted_f = wanted.astype(F32)
    square[...] = jnp.zeros_like(square)
    loads[4].wait()
    square[0:OWN, 0:80] = res_ref[...]
    loads[5].wait()
    square[64 : 64 + OWN, 0:80] = stab_ref[...]
    turned = square[...].T
    faces = jnp.zeros((ROWS, 128), F32)
    for j in range(PARTS):
        block = turned[j * ROWS : (j + 1) * ROWS]
        block = pltpu.roll(block, j * OWN, 1) if j else block
        faces = jnp.where(jnp.logical_and(low >= j * OWN, low < (j + 1) * OWN), block, faces)
    first[SELF, 0:ROWS] = faces
    first[SELF, ROWS : ROWS + 8] = jnp.broadcast_to(wanted_f[:, :128], (8, 128))

    loads[0].wait()
    res_rows = jnp.concatenate([vol_res[...], jnp.zeros((124, 320), BF16)], axis=0)
    across = (((1,), (1,)), ((), ()))
    loads[1].wait()
    local = lax.dot_general(inv[0], res_rows, across, preferred_element_type=F32)
    at = lax.broadcasted_iota(I32, local.shape, 1)
    for e in range(1, 4):
        local = jnp.where(at == e, lax.dot_general(inv[e], res_rows, across, preferred_element_type=F32), local)
    local = jnp.concatenate([local, jnp.zeros((64, 128), F32)], axis=0)
    local = jnp.concatenate([local[n * 128 : (n + 1) * 128].T[0:ROWS] for n in range(3)], axis=1)
    local_rows = local[0:8]
    level = lax.broadcasted_iota(I32, (ROWS, 320), 0)
    local = jnp.concatenate(
        [jnp.where(level == e, local[:, 0:320], 0.0).astype(BF16) for e in range(4)], axis=1
    )
    pl.semaphore_wait(barrier, SELF)
    send(0, first)
    loads[2].wait()
    load = jnp.zeros((ROWS, 480), F32)
    for e in range(4):
        load = load + jnp.dot(local[:, e * 320 : (e + 1) * 320], down[e], preferred_element_type=F32)
    load = jnp.concatenate([load, jnp.zeros((ROWS, 32), F32)], axis=1)
    load = jnp.concatenate([load, jnp.zeros((112, 512), F32)], axis=0)
    load = jnp.concatenate([load[:, n * 128 : (n + 1) * 128].T for n in range(4)], axis=0)
    own = jnp.zeros((ROWS, 128), F32)
    for j in range(PARTS):
        for k in range(6):
            begin = k * 80 + j * ROWS
            place = j * SLOTS + k * 4
            block = load[begin : begin + ROWS]
            block = pltpu.roll(block, place, 1) if place else block
            own = jnp.where(jnp.logical_and(small >= place, small < place + 4), block, own)
    tiles[0, SELF] = own.astype(BF16)

    send(1, tiles.at[0])

    loads[6].wait()

    def condense(e, carry):
        block = jnp.dot(inv[e], up[e], preferred_element_type=F32).astype(BF16)
        block = jnp.concatenate([block, jnp.zeros((320, 32), BF16)], axis=1)
        couple[e] = block
        schur[e] = lax.dot_general(
            down[e], block, (((0,), (0,)), ((), ())), preferred_element_type=F32
        ).astype(BF16)
        return carry

    lax.fori_loop(0, 4, condense, 0)

    arrive(0, first, recv_sem)
    eight = lax.broadcasted_iota(I32, (8, 128), 0)
    for base in range(0, KINDS, 8):
        rows = jnp.zeros((8, 128), F32)
        for n in range(8):
            rows = jnp.where(eight == n, first[base + n, ROWS : ROWS + 8], rows)
        square[base : base + 8] = rows
    square[KINDS:32] = jnp.zeros((32 - KINDS, 128), F32)
    held = square[...].T
    slot_row = lax.broadcasted_iota(I32, (SLOTS, 128), 0).astype(F32)
    wide_slot = jnp.broadcast_to(wanted_f[:, :128], (SLOTS, 128))
    wide_face = jnp.broadcast_to(wanted_f[:, 128:], (SLOTS, 128))
    slot_sum = jnp.zeros((SLOTS, 128), F32)
    face_total = jnp.zeros((SLOTS, 128), F32)
    least = jnp.full((SLOTS, 128), 4096.0, F32)
    for n in range(KINDS):
        column = jnp.broadcast_to(held[0:SLOTS, n : n + 1], (SLOTS, 128))
        code = slot_row + 32.0 * n
        slot_sum = slot_sum + jnp.where(column == wide_slot, code, 0.0)
        if n < SELF and PEERS[n][0] > 0:
            continue
        hit = column == wide_face
        face_total = face_total + jnp.where(hit, code, 0.0)
        least = jnp.minimum(least, jnp.where(hit, code, 4096.0))
    slot_sum = jnp.sum(slot_sum, axis=0, keepdims=True) - (SELF * 32 + index[:, :128]).astype(F32)
    face_total = jnp.sum(face_total, axis=0, keepdims=True)
    least = jnp.min(least, axis=0, keepdims=True)
    face_code = jnp.where(lane[:, :128] < 64, least, face_total - least)
    code = jnp.concatenate([slot_sum, face_code], axis=1).astype(I32)
    kinds = jnp.where(used, lax.shift_right_arithmetic(code, 5), -1)
    row = jnp.where(used, part * SLOTS + lax.bitwise_and(code, 31), -1)
    deep = lax.broadcasted_iota(I32, (128, 256), 0)
    pick[...] = jnp.where(deep == row, 1.0, 0.0).astype(BF16)
    kind_row[...] = jnp.broadcast_to(kinds, (ROWS, 256))

    owner = jnp.full((1, 128), -1, I32)
    place = jnp.zeros((1, 128), I32)
    sources = [n for n in range(SELF) if PEERS[n][0] >= 0] + [SELF]
    for n in sources:
        shift, turn = PEERS[n] if n < SELF else (0, 0)
        base = lax.rem(group - shift + groups, groups) * group_faces + lax.rem(member - turn + members, members) * OWN
        offset = wanted[:, :128] - base
        hit = jnp.logical_and(offset >= 0, offset < OWN)
        owner = jnp.where(hit, n, owner)
        place = jnp.where(hit, offset, place)
    place = part[:, :128] * OWN + place
    slim = lax.broadcasted_iota(I32, (128, 128), 0)
    face_pick[:, 0:128] = jnp.where(slim == place, 1.0, 0.0).astype(BF16)
    face_pick[:, 128:256] = jnp.where(slim == place + 64, 1.0, 0.0).astype(BF16)
    sent = jnp.concatenate([first[n, 0:ROWS] for n in sources], axis=0)
    high = sent.astype(BF16)
    rest = (sent - high.astype(F32)).astype(BF16)
    found = jnp.dot(high, face_pick[...], preferred_element_type=F32)
    found = found + jnp.dot(rest, face_pick[...], preferred_element_type=F32)
    owner_rows = jnp.broadcast_to(owner, (ROWS, 128))
    right = jnp.zeros((ROWS, 128), F32)
    stab = jnp.zeros((ROWS, 128), F32)
    for at, n in enumerate(sources):
        block = found[at * ROWS : (at + 1) * ROWS]
        right = jnp.where(owner_rows == n, block[:, :128], right)
        stab = jnp.where(owner_rows == n, block[:, 128:], stab)
    scale = 1.0 / jnp.where(owner_rows >= 0, stab, 1.0)
    face_stab = pltpu.roll(first[SELF, 0:ROWS], 64, 1)
    face_scale = 1.0 / jnp.where(small < OWN * PARTS, face_stab, 1.0)

    def gathered(phase, columns):
        stack = tiles[phase].reshape(KINDS * ROWS, 128)
        found = jnp.dot(stack, pick[:, columns], preferred_element_type=F32)
        kinds = kind_row[:, columns]
        total = []
        for begin in range(0, KINDS, 6):
            some = jnp.zeros((ROWS, 128), F32)
            for n in range(begin, begin + 6):
                some = jnp.where(kinds == n, found[n * ROWS : (n + 1) * ROWS], some)
            total.append(some)
        return (total[0] + total[1]) + (total[2] + total[3])

    def partners(phase):
        return gathered(phase, slice(0, 128))

    def face_sum(phase):
        both = gathered(phase, slice(128, 256))
        return both + pltpu.roll(both, 64, 1)

    def fits(place):
        return jnp.logical_and(small >= place, small < place + 4)

    odd = lax.bitwise_and(small, 1) == 1

    def spread(lam):
        for k in range(6):
            for j in range(PARTS):
                block = jnp.take_along_axis(lam, fourth + (j * SLOTS + k * 4), axis=1)
                begin = k * 80 + j * ROWS
                rhs_mat[begin : begin + ROWS] = jnp.where(odd, 0.0, block).astype(BF16)
                rhs_mat[512 + begin : 512 + begin + ROWS] = jnp.where(odd, block, 0.0).astype(BF16)

    def products(blocks):
        left, right = (
            jnp.dot(jnp.concatenate([blocks[e], blocks[e + 1]], axis=1), rhs_mat[...], preferred_element_type=F32)
            for e in (0, 2)
        )
        return jnp.where(lax.bitwise_and(lax.broadcasted_iota(I32, left.shape, 1), 3) < 2, left, right)

    def image():
        product = products(schur)
        tile = []
        for j in range(PARTS):
            some = jnp.zeros((ROWS, 128), F32)
            for k in range(6):
                begin = k * 80 + j * ROWS
                some = jnp.where(fits(j * SLOTS + k * 4), product[begin : begin + ROWS], some)
            tile.append(some)
        return (tile[0] + tile[1]) + (tile[2] + tile[3]) + tile[4]

    arrive(1, tiles.at[0], recv_sem)
    right = right - (own + partners(0))
    spread(right * scale)
    for sweep in range(1, SWEEPS):
        own = image()
        tiles[sweep, SELF] = own.astype(BF16)
        send(sweep + 1, tiles.at[sweep])
        if sweep == 1:
            face_right = first[SELF, 0:ROWS] - face_sum(0)
        arrive(sweep + 1, tiles.at[sweep], recv_sem)
        spread((right + own + partners(sweep)) * scale)

    back = products(couple)
    face_now = (face_right + face_sum(SWEEPS - 1)) * face_scale
    for j in range(PARTS):
        block = pltpu.roll(face_now, 128 - j * OWN, 1) if j else face_now
        square[j * ROWS : (j + 1) * ROWS] = block
    trace_out[...] = square[...].T[0:ROWS]
    back = jnp.concatenate([back, jnp.zeros((64, 128), F32)], axis=0)
    for n in range(3):
        columns = slice(n * 128, (n + 1) * 128)
        vol_out[:, columns] = local_rows[:, columns] - back[columns].T[0:8]

    arrive(0, first, send_sem)
    for phase in range(SWEEPS):
        arrive(phase + 1, tiles.at[phase], send_sem)


def write(trace_in, vol_in, trace_out, vol_out):
    trace_out[...] = trace_in[0:OWN, 0:80]
    vol_out[...] = vol_in[0:4, 0:320]


def solution(mesh):
    groups, members = mesh.shape["elem"], mesh.shape["face"]
    spec2, spec3 = P(("elem", "face"), None), P(("elem", "face"), None, None)

    def local(vol_inverse, vol_from_trace, trace_from_vol, vol_residual, face_ids, trace_residual, stabilization):
        vmem, hbm = pl.BlockSpec(memory_space=pltpu.VMEM), pl.BlockSpec(memory_space=pl.ANY)
        trace, vol = pl.pallas_call(
            functools.partial(kernel, groups, members),
            out_shape=(pltpu.VMEM((ROWS, 128), F32), pltpu.VMEM((8, 384), F32)),
            in_specs=[hbm] * 7,
            out_specs=(vmem, vmem),
            scratch_shapes=[
                pltpu.SMEM((4, 6), I32),
                pltpu.VMEM((4, 320), BF16),
                pltpu.VMEM((OWN, 80), F32),
                pltpu.VMEM((OWN, 80), F32),
                pltpu.VMEM((4, 320, 320), BF16),
                pltpu.VMEM((4, 320, 480), BF16),
                pltpu.VMEM((4, 320, 480), BF16),
                pltpu.VMEM((4, 320, 512), BF16),
                pltpu.VMEM((4, 480, 512), BF16),
                pltpu.VMEM((1024, 128), BF16),
                pltpu.VMEM((KINDS, ROWS + 8, 128), F32),
                pltpu.VMEM((SWEEPS, KINDS, ROWS, 128), BF16),
                pltpu.VMEM((128, 256), BF16),
                pltpu.VMEM((128, 256), BF16),
                pltpu.VMEM((ROWS, 256), I32),
                pltpu.VMEM((128, 128), F32),
                pltpu.SemaphoreType.DMA((7,)),
                pltpu.SemaphoreType.DMA((SWEEPS + 1,)),
                pltpu.SemaphoreType.DMA((SWEEPS + 1,)),
            ],
            compiler_params=pltpu.CompilerParams(collective_id=0, has_side_effects=True),
            name="newton",
        )(
            face_ids, vol_inverse, vol_from_trace, jnp.swapaxes(trace_from_vol, 1, 2), vol_residual,
            trace_residual, stabilization,
        )
        return pl.pallas_call(
            write,
            out_shape=(
                jax.ShapeDtypeStruct(trace_residual.shape, F32),
                jax.ShapeDtypeStruct(vol_residual.shape, F32),
            ),
            in_specs=[vmem, vmem],
            out_specs=(vmem, vmem),
            name="write",
        )(pltpu.with_memory_space_constraint(trace, pltpu.VMEM), pltpu.with_memory_space_constraint(vol, pltpu.VMEM))

    return jax.shard_map(
        local,
        mesh=mesh,
        in_specs=(spec3, spec3, spec3, spec2, spec2, spec2, spec2),
        out_specs=(spec2, spec2),
        check_vma=False,
    )
```

```python
import functools

import jax
import jax.numpy as jnp
from jax import lax
from jax.experimental import pallas as pl
from jax.experimental.pallas import tpu as pltpu
from jax.sharding import PartitionSpec as P

MESH = pl.DeviceIdType.MESH
F32, BF16, I32 = jnp.float32, jnp.bfloat16, jnp.int32
SWEEPS = 5
ROWS, PARTS, SLOTS, OWN = 16, 5, 24, 12
TURNS = (4, 3, 5, 2, 6, 1, 7)
PEERS = tuple((1, i) for i in TURNS + (0,)) + tuple((-1, i) for i in TURNS + (0,)) + tuple((0, i) for i in TURNS)
SELF = len(PEERS)
KINDS = SELF + 1


def kernel(groups, members, ids_hbm, inv_hbm, up_hbm, down_hbm, vol_hbm, res_hbm, stab_hbm, trace_out, vol_out,
           ids, vol_res, res_ref, stab_ref, inv, up, down, couple, schur, first, tiles, pick, face_pick,
           kind_row, square, load_sem, send_sem, recv_sem):
    group, member = lax.axis_index("elem"), lax.axis_index("face")
    group_faces = OWN * members

    def device(shift, turn):
        return (lax.rem(group + shift + groups, groups), lax.rem(member + turn + members, members))

    barrier = pltpu.get_barrier_semaphore()
    for shift, turn in PEERS:
        pl.semaphore_signal(barrier, inc=1, device_id=device(shift, turn), device_id_type=MESH)
    pairs = ((vol_hbm, vol_res), (inv_hbm, inv), (down_hbm, down), (ids_hbm, ids), (res_hbm, res_ref),
             (stab_hbm, stab_ref), (up_hbm, up))
    loads = [pltpu.make_async_copy(src, dst, load_sem.at[n]) for n, (src, dst) in enumerate(pairs)]
    for copy in loads:
        copy.start()

    lane = lax.broadcasted_iota(I32, (1, 256), 1)

    def steps(x, width, count):
        return sum((x >= width * n).astype(I32) for n in range(1, count))

    half = lane >= 128
    inner = jnp.where(half, lax.bitwise_and(lane, 63), lane)
    part = jnp.where(half, steps(inner, OWN, PARTS), steps(inner, SLOTS, PARTS))
    index = inner - part * jnp.where(half, OWN, SLOTS)
    used = inner < jnp.where(half, OWN * PARTS, SLOTS * PARTS)
    small = lax.broadcasted_iota(I32, (ROWS, 128), 1)
    low = lax.bitwise_and(small, 63)
    across_rows, across_lanes = lax.broadcasted_iota(I32, (8, 128), 0), lax.broadcasted_iota(I32, (8, 128), 1)
    upper = across_rows < 4

    def spot(k, j):
        group = k * PARTS + j
        return (j * 3 + k // 2) * 8, group // 8, group % 8 * ROWS

    def to_rows(tile):
        turned = jnp.concatenate([tile, jnp.zeros((112, 128), F32)], axis=0).T
        rows = [jnp.zeros((8, 128), F32)] * 4
        for k in range(6):
            for j in range(PARTS):
                begin, n, place = spot(k, j)
                block = turned[begin : begin + 8]
                block = pltpu.roll(block, place, 1) if place else block
                here = jnp.logical_and(across_lanes >= place, across_lanes < place + ROWS)
                here = jnp.logical_and(here, upper if k % 2 == 0 else across_rows >= 4)
                rows[n] = jnp.where(here, block, rows[n])
        rows = jnp.concatenate([row + pltpu.roll(row, 4, 0) for row in rows], axis=1)
        return jnp.concatenate([rows, rows], axis=0).astype(BF16)

    def to_tile(rows):
        blocks = []
        for j in range(PARTS):
            for k in range(0, 6, 2):
                pair = []
                for odd in range(2):
                    _, n, place = spot(k + odd, j)
                    block = rows[:, n * 128 : (n + 1) * 128]
                    pair.append(pltpu.roll(block, 128 - place, 1) if place else block)
                blocks.append(jnp.where(upper, pair[0], pair[1]))
        blocks.append(jnp.zeros((8, 128), F32))
        return jnp.concatenate(blocks, axis=0).T[0:ROWS]

    def products(rows, blocks):
        total = jnp.dot(rows, blocks[0], preferred_element_type=F32)[0:8]
        of = lax.bitwise_and(lax.broadcasted_iota(I32, total.shape, 0), 3)
        for e in range(1, 4):
            total = jnp.where(of == e, jnp.dot(rows, blocks[e], preferred_element_type=F32)[0:8], total)
        return total


    def send(phase, ref):
        for n, (shift, turn) in enumerate(PEERS):
            pltpu.make_async_remote_copy(
                src_ref=ref.at[SELF],
                dst_ref=ref.at[n],
                send_sem=send_sem.at[phase],
                recv_sem=recv_sem.at[phase],
                device_id=device(shift, turn),
                device_id_type=MESH,
            ).start()

    def arrive(phase, ref, sem):
        some = ref.at[pl.ds(0, SELF)]
        pltpu.make_async_copy(some, some, sem.at[phase]).wait()

    loads[3].wait()
    own_base = group * group_faces + member * OWN
    wanted = own_base + index
    for s in range(SLOTS):
        wanted = jnp.where(jnp.logical_and(lane < 128, index == s), ids[s % 4, s // 4], wanted)
    wanted = jnp.where(used, wanted, -1)
    wanted_f = wanted.astype(F32)
    square[...] = jnp.zeros_like(square)
    loads[4].wait()
    square[0:OWN, 0:80] = res_ref[...]
    loads[5].wait()
    square[64 : 64 + OWN, 0:80] = stab_ref[...]
    turned = square[...].T
    faces = jnp.zeros((ROWS, 128), F32)
    for j in range(PARTS):
        block = turned[j * ROWS : (j + 1) * ROWS]
        block = pltpu.roll(block, j * OWN, 1) if j else block
        faces = jnp.where(jnp.logical_and(low >= j * OWN, low < (j + 1) * OWN), block, faces)
    first[SELF, 0:ROWS] = faces
    first[SELF, ROWS : ROWS + 8] = jnp.broadcast_to(wanted_f[:, :128], (8, 128))

    loads[0].wait()
    res_rows = jnp.concatenate([vol_res[...], vol_res[...], jnp.zeros((120, 320), BF16)], axis=0)
    across = (((1,), (1,)), ((), ()))
    loads[1].wait()
    local = lax.dot_general(inv[0], res_rows, across, preferred_element_type=F32)
    at = lax.bitwise_and(lax.broadcasted_iota(I32, local.shape, 1), 3)
    for e in range(1, 4):
        local = jnp.where(at == e, lax.dot_general(inv[e], res_rows, across, preferred_element_type=F32), local)
    local = jnp.concatenate([local, jnp.zeros((64, 128), F32)], axis=0)
    local = jnp.concatenate([local[n * 128 : (n + 1) * 128].T[0:ROWS] for n in range(3)], axis=1)
    local_rows = local[0:8]
    level = lax.bitwise_and(lax.broadcasted_iota(I32, (ROWS, 320), 0), 3)
    pl.semaphore_wait(barrier, SELF)
    send(0, first)
    loads[2].wait()
    load = jnp.zeros((ROWS, 480), F32)
    for e in range(4):
        row = jnp.where(level == e, local[:, 0:320], 0.0).astype(BF16)
        load = load + jnp.dot(row, down[e], preferred_element_type=F32)
    own = to_tile(jnp.concatenate([load[0:8], jnp.zeros((8, 32), F32)], axis=1))
    tiles[0, SELF] = own.astype(BF16)

    send(1, tiles.at[0])

    loads[6].wait()

    def condense(e, carry):
        block = lax.dot_general(up[e], inv[e], (((0,), (1,)), ((), ())), preferred_element_type=F32).astype(BF16)
        block = jnp.concatenate([block, jnp.zeros((32, 320), BF16)], axis=0)
        couple[e] = block
        block = jnp.dot(block, down[e], preferred_element_type=F32).astype(BF16)
        schur[e] = jnp.concatenate([block, jnp.zeros((512, 32), BF16)], axis=1)
        return carry

    lax.fori_loop(0, 4, condense, 0)

    arrive(0, first, recv_sem)
    eight = lax.broadcasted_iota(I32, (8, 128), 0)
    for base in range(0, KINDS, 8):
        rows = jnp.zeros((8, 128), F32)
        for n in range(8):
            rows = jnp.where(eight == n, first[base + n, ROWS : ROWS + 8], rows)
        square[base : base + 8] = rows
    square[KINDS:32] = jnp.zeros((32 - KINDS, 128), F32)
    held = square[...].T
    slot_row = lax.broadcasted_iota(I32, (SLOTS, 128), 0).astype(F32)
    wide_slot = jnp.broadcast_to(wanted_f[:, :128], (SLOTS, 128))
    wide_face = jnp.broadcast_to(wanted_f[:, 128:], (SLOTS, 128))
    slot_sum = jnp.zeros((SLOTS, 128), F32)
    face_total = jnp.zeros((SLOTS, 128), F32)
    least = jnp.full((SLOTS, 128), 4096.0, F32)
    for n in range(KINDS):
        column = jnp.broadcast_to(held[0:SLOTS, n : n + 1], (SLOTS, 128))
        code = slot_row + 32.0 * n
        slot_sum = slot_sum + jnp.where(column == wide_slot, code, 0.0)
        if n < SELF and PEERS[n][0] > 0:
            continue
        hit = column == wide_face
        face_total = face_total + jnp.where(hit, code, 0.0)
        least = jnp.minimum(least, jnp.where(hit, code, 4096.0))
    slot_sum = jnp.sum(slot_sum, axis=0, keepdims=True) - (SELF * 32 + index[:, :128]).astype(F32)
    face_total = jnp.sum(face_total, axis=0, keepdims=True)
    least = jnp.min(least, axis=0, keepdims=True)
    face_code = jnp.where(lane[:, :128] < 64, least, face_total - least)
    code = jnp.concatenate([slot_sum, face_code], axis=1).astype(I32)
    kinds = jnp.where(used, lax.shift_right_arithmetic(code, 5), -1)
    row = jnp.where(used, part * SLOTS + lax.bitwise_and(code, 31), -1)
    deep = lax.broadcasted_iota(I32, (128, 256), 0)
    pick[...] = jnp.where(deep == row, 1.0, 0.0).astype(BF16)
    kind_row[...] = jnp.broadcast_to(kinds, (ROWS, 256))

    owner = jnp.full((1, 128), -1, I32)
    place = jnp.zeros((1, 128), I32)
    sources = [n for n in range(SELF) if PEERS[n][0] >= 0] + [SELF]
    for n in sources:
        shift, turn = PEERS[n] if n < SELF else (0, 0)
        base = lax.rem(group - shift + groups, groups) * group_faces + lax.rem(member - turn + members, members) * OWN
        offset = wanted[:, :128] - base
        hit = jnp.logical_and(offset >= 0, offset < OWN)
        owner = jnp.where(hit, n, owner)
        place = jnp.where(hit, offset, place)
    place = part[:, :128] * OWN + place
    slim = lax.broadcasted_iota(I32, (128, 128), 0)
    face_pick[:, 0:128] = jnp.where(slim == place, 1.0, 0.0).astype(BF16)
    face_pick[:, 128:256] = jnp.where(slim == place + 64, 1.0, 0.0).astype(BF16)
    sent = jnp.concatenate([first[n, 0:ROWS] for n in sources], axis=0)
    high = sent.astype(BF16)
    rest = (sent - high.astype(F32)).astype(BF16)
    found = jnp.dot(high, face_pick[...], preferred_element_type=F32)
    found = found + jnp.dot(rest, face_pick[...], preferred_element_type=F32)
    owner_rows = jnp.broadcast_to(owner, (ROWS, 128))
    right = jnp.zeros((ROWS, 128), F32)
    stab = jnp.zeros((ROWS, 128), F32)
    for at, n in enumerate(sources):
        block = found[at * ROWS : (at + 1) * ROWS]
        right = jnp.where(owner_rows == n, block[:, :128], right)
        stab = jnp.where(owner_rows == n, block[:, 128:], stab)
    scale = 1.0 / jnp.where(owner_rows >= 0, stab, 1.0)
    face_stab = pltpu.roll(first[SELF, 0:ROWS], 64, 1)
    face_scale = 1.0 / jnp.where(small < OWN * PARTS, face_stab, 1.0)

    def gathered(phase, columns):
        stack = tiles[phase].reshape(KINDS * ROWS, 128)
        found = jnp.dot(stack, pick[:, columns], preferred_element_type=F32)
        kinds = kind_row[:, columns]
        total = []
        for begin in range(0, KINDS, 6):
            some = jnp.zeros((ROWS, 128), F32)
            for n in range(begin, begin + 6):
                some = jnp.where(kinds == n, found[n * ROWS : (n + 1) * ROWS], some)
            total.append(some)
        return (total[0] + total[1]) + (total[2] + total[3])

    def partners(phase):
        return gathered(phase, slice(0, 128))

    def face_sum(phase):
        both = gathered(phase, slice(128, 256))
        return both + pltpu.roll(both, 64, 1)

    arrive(1, tiles.at[0], recv_sem)
    right = right - (own + partners(0))
    rows = to_rows(right * scale)
    for sweep in range(1, SWEEPS):
        own = to_tile(products(rows, schur))
        tiles[sweep, SELF] = own.astype(BF16)
        send(sweep + 1, tiles.at[sweep])
        if sweep == 1:
            face_right = first[SELF, 0:ROWS] - face_sum(0)
        arrive(sweep + 1, tiles.at[sweep], recv_sem)
        rows = to_rows((right + own + partners(sweep)) * scale)

    back = products(rows, couple)
    vol_out[...] = local_rows - jnp.concatenate([back, jnp.zeros((8, 64), F32)], axis=1)
    face_now = (face_right + face_sum(SWEEPS - 1)) * face_scale
    for j in range(PARTS):
        block = pltpu.roll(face_now, 128 - j * OWN, 1) if j else face_now
        square[j * ROWS : (j + 1) * ROWS] = block
    trace_out[...] = square[...].T[0:ROWS]

    arrive(0, first, send_sem)
    for phase in range(SWEEPS):
        arrive(phase + 1, tiles.at[phase], send_sem)


def write(trace_in, vol_in, trace_out, vol_out):
    trace_out[...] = trace_in[0:OWN, 0:80]
    vol_out[...] = vol_in[0:4, 0:320]


def solution(mesh):
    groups, members = mesh.shape["elem"], mesh.shape["face"]
    spec2, spec3 = P(("elem", "face"), None), P(("elem", "face"), None, None)

    def local(vol_inverse, vol_from_trace, trace_from_vol, vol_residual, face_ids, trace_residual, stabilization):
        vmem, hbm = pl.BlockSpec(memory_space=pltpu.VMEM), pl.BlockSpec(memory_space=pl.ANY)
        trace, vol = pl.pallas_call(
            functools.partial(kernel, groups, members),
            out_shape=(pltpu.VMEM((ROWS, 128), F32), pltpu.VMEM((8, 384), F32)),
            in_specs=[hbm] * 7,
            out_specs=(vmem, vmem),
            scratch_shapes=[
                pltpu.SMEM((4, 6), I32),
                pltpu.VMEM((4, 320), BF16),
                pltpu.VMEM((OWN, 80), F32),
                pltpu.VMEM((OWN, 80), F32),
                pltpu.VMEM((4, 320, 320), BF16),
                pltpu.VMEM((4, 320, 480), BF16),
                pltpu.VMEM((4, 320, 480), BF16),
                pltpu.VMEM((4, 512, 320), BF16),
                pltpu.VMEM((4, 512, 512), BF16),
                pltpu.VMEM((KINDS, ROWS + 8, 128), F32),
                pltpu.VMEM((SWEEPS, KINDS, ROWS, 128), BF16),
                pltpu.VMEM((128, 256), BF16),
                pltpu.VMEM((128, 256), BF16),
                pltpu.VMEM((ROWS, 256), I32),
                pltpu.VMEM((128, 128), F32),
                pltpu.SemaphoreType.DMA((7,)),
                pltpu.SemaphoreType.DMA((SWEEPS + 1,)),
                pltpu.SemaphoreType.DMA((SWEEPS + 1,)),
            ],
            compiler_params=pltpu.CompilerParams(collective_id=0, has_side_effects=True),
            name="newton",
        )(
            face_ids, vol_inverse, vol_from_trace, jnp.swapaxes(trace_from_vol, 1, 2), vol_residual,
            trace_residual, stabilization,
        )
        return pl.pallas_call(
            write,
            out_shape=(
                jax.ShapeDtypeStruct(trace_residual.shape, F32),
                jax.ShapeDtypeStruct(vol_residual.shape, F32),
            ),
            in_specs=[vmem, vmem],
            out_specs=(vmem, vmem),
            name="write",
        )(pltpu.with_memory_space_constraint(trace, pltpu.VMEM), pltpu.with_memory_space_constraint(vol, pltpu.VMEM))

    return jax.shard_map(
        local,
        mesh=mesh,
        in_specs=(spec3, spec3, spec3, spec2, spec2, spec2, spec2),
        out_specs=(spec2, spec2),
        check_vma=False,
    )
```

```python
import functools

import jax
import jax.numpy as jnp
from jax import lax
from jax.experimental import pallas as pl
from jax.experimental.pallas import tpu as pltpu
from jax.sharding import PartitionSpec as P

MESH = pl.DeviceIdType.MESH
F32, BF16, I32 = jnp.float32, jnp.bfloat16, jnp.int32
SWEEPS = 5
ROWS, PARTS, SLOTS, OWN = 16, 5, 24, 12
TURNS = (4, 3, 5, 2, 6, 1, 7)
PEERS = tuple((1, i) for i in TURNS + (0,)) + tuple((-1, i) for i in TURNS + (0,)) + tuple((0, i) for i in TURNS)
SELF = len(PEERS)
FAR = 16
KINDS = SELF + 1


def kernel(groups, members, ids_hbm, inv_hbm, up_hbm, down_hbm, vol_hbm, res_hbm, stab_hbm, trace_out, vol_out,
           ids, vol_res, res_ref, stab_ref, inv, up, down, couple, schur, first, tiles, pick, face_pick,
           kind_row, square, load_sem, send_sem, recv_sem):
    group, member = lax.axis_index("elem"), lax.axis_index("face")
    group_faces = OWN * members

    def device(shift, turn):
        return (lax.rem(group + shift + groups, groups), lax.rem(member + turn + members, members))

    barrier = pltpu.get_barrier_semaphore()
    for shift, turn in PEERS:
        pl.semaphore_signal(barrier, inc=1, device_id=device(shift, turn), device_id_type=MESH)
    pairs = ((vol_hbm, vol_res), (inv_hbm, inv), (down_hbm, down), (ids_hbm, ids), (res_hbm, res_ref),
             (stab_hbm, stab_ref), (up_hbm, up))
    loads = [pltpu.make_async_copy(src, dst, load_sem.at[n]) for n, (src, dst) in enumerate(pairs)]
    for copy in loads:
        copy.start()

    lane = lax.broadcasted_iota(I32, (1, 256), 1)

    def steps(x, width, count):
        return sum((x >= width * n).astype(I32) for n in range(1, count))

    half = lane >= 128
    inner = jnp.where(half, lax.bitwise_and(lane, 63), lane)
    part = jnp.where(half, steps(inner, OWN, PARTS), steps(inner, SLOTS, PARTS))
    index = inner - part * jnp.where(half, OWN, SLOTS)
    used = inner < jnp.where(half, OWN * PARTS, SLOTS * PARTS)
    small = lax.broadcasted_iota(I32, (ROWS, 128), 1)
    low = lax.bitwise_and(small, 63)
    across_rows, across_lanes = lax.broadcasted_iota(I32, (8, 128), 0), lax.broadcasted_iota(I32, (8, 128), 1)
    upper = across_rows < 4

    def spot(k, j):
        group = k * PARTS + j
        return (j * 3 + k // 2) * 8, group // 8, group % 8 * ROWS

    def to_rows(tile):
        turned = jnp.concatenate([tile, jnp.zeros((112, 128), F32)], axis=0).T
        rows = [jnp.zeros((8, 128), F32)] * 4
        for k in range(6):
            for j in range(PARTS):
                begin, n, place = spot(k, j)
                block = turned[begin : begin + 8]
                block = pltpu.roll(block, place, 1) if place else block
                here = jnp.logical_and(across_lanes >= place, across_lanes < place + ROWS)
                here = jnp.logical_and(here, upper if k % 2 == 0 else across_rows >= 4)
                rows[n] = jnp.where(here, block, rows[n])
        rows = jnp.concatenate([row + pltpu.roll(row, 4, 0) for row in rows], axis=1)
        return jnp.concatenate([rows, rows], axis=0).astype(BF16)

    def to_tile(rows):
        blocks = []
        for j in range(PARTS):
            for k in range(0, 6, 2):
                pair = []
                for odd in range(2):
                    _, n, place = spot(k + odd, j)
                    block = rows[:, n * 128 : (n + 1) * 128]
                    pair.append(pltpu.roll(block, 128 - place, 1) if place else block)
                blocks.append(jnp.where(upper, pair[0], pair[1]))
        blocks.append(jnp.zeros((8, 128), F32))
        return jnp.concatenate(blocks, axis=0).T[0:ROWS]

    def products(rows, blocks):
        total = jnp.dot(rows, blocks[0], preferred_element_type=F32)[0:8]
        of = lax.bitwise_and(lax.broadcasted_iota(I32, total.shape, 0), 3)
        for e in range(1, 4):
            total = jnp.where(of == e, jnp.dot(rows, blocks[e], preferred_element_type=F32)[0:8], total)
        return total


    def send(phase, ref):
        for n, (shift, turn) in enumerate(PEERS):
            pltpu.make_async_remote_copy(
                src_ref=ref.at[SELF],
                dst_ref=ref.at[n],
                send_sem=send_sem.at[phase],
                recv_sem=recv_sem.at[phase, int(n >= FAR)],
                device_id=device(shift, turn),
                device_id_type=MESH,
            ).start()

    def leave(phase, ref):
        some = ref.at[pl.ds(0, SELF)]
        pltpu.make_async_copy(some, some, send_sem.at[phase]).wait()

    def arrive(phase, ref, near):
        some = ref.at[pl.ds(FAR, SELF - FAR) if near else pl.ds(0, FAR)]
        pltpu.make_async_copy(some, some, recv_sem.at[phase, near]).wait()

    loads[3].wait()
    own_base = group * group_faces + member * OWN
    wanted = own_base + index
    for s in range(SLOTS):
        wanted = jnp.where(jnp.logical_and(lane < 128, index == s), ids[s % 4, s // 4], wanted)
    wanted = jnp.where(used, wanted, -1)
    wanted_f = wanted.astype(F32)
    square[...] = jnp.zeros_like(square)
    loads[4].wait()
    square[0:OWN, 0:80] = res_ref[...]
    loads[5].wait()
    square[64 : 64 + OWN, 0:80] = stab_ref[...]
    turned = square[...].T
    faces = jnp.zeros((ROWS, 128), F32)
    for j in range(PARTS):
        block = turned[j * ROWS : (j + 1) * ROWS]
        block = pltpu.roll(block, j * OWN, 1) if j else block
        faces = jnp.where(jnp.logical_and(low >= j * OWN, low < (j + 1) * OWN), block, faces)
    first[SELF, 0:ROWS] = faces
    first[SELF, ROWS : ROWS + 8] = jnp.broadcast_to(wanted_f[:, :128], (8, 128))

    loads[0].wait()
    res_rows = jnp.concatenate([vol_res[...], vol_res[...], jnp.zeros((120, 320), BF16)], axis=0)
    across = (((1,), (1,)), ((), ()))
    loads[1].wait()
    local = lax.dot_general(inv[0], res_rows, across, preferred_element_type=F32)
    at = lax.bitwise_and(lax.broadcasted_iota(I32, local.shape, 1), 3)
    for e in range(1, 4):
        local = jnp.where(at == e, lax.dot_general(inv[e], res_rows, across, preferred_element_type=F32), local)
    local = jnp.concatenate([local, jnp.zeros((64, 128), F32)], axis=0)
    local = jnp.concatenate([local[n * 128 : (n + 1) * 128].T[0:ROWS] for n in range(3)], axis=1)
    local_rows = local[0:8]
    level = lax.bitwise_and(lax.broadcasted_iota(I32, (ROWS, 320), 0), 3)
    loads[2].wait()
    load = jnp.zeros((ROWS, 480), F32)
    for e in range(4):
        row = jnp.where(level == e, local[:, 0:320], 0.0).astype(BF16)
        load = load + jnp.dot(row, down[e], preferred_element_type=F32)
    own = to_tile(jnp.concatenate([load[0:8], jnp.zeros((8, 32), F32)], axis=1))
    tiles[0, SELF] = own.astype(BF16)

    pl.semaphore_wait(barrier, SELF)
    send(0, first)
    send(1, tiles.at[0])

    loads[6].wait()

    def condense(e, carry):
        block = lax.dot_general(up[e], inv[e], (((0,), (1,)), ((), ())), preferred_element_type=F32).astype(BF16)
        block = jnp.concatenate([block, jnp.zeros((32, 320), BF16)], axis=0)
        couple[e] = block
        block = jnp.dot(block, down[e], preferred_element_type=F32).astype(BF16)
        schur[e] = jnp.concatenate([block, jnp.zeros((512, 32), BF16)], axis=1)
        return carry

    lax.fori_loop(0, 4, condense, 0)

    owner = jnp.full((1, 128), -1, I32)
    place = jnp.zeros((1, 128), I32)
    sources = [n for n in range(SELF) if PEERS[n][0] >= 0] + [SELF]
    for n in sources:
        shift, turn = PEERS[n] if n < SELF else (0, 0)
        base = lax.rem(group - shift + groups, groups) * group_faces + lax.rem(member - turn + members, members) * OWN
        offset = wanted[:, :128] - base
        hit = jnp.logical_and(offset >= 0, offset < OWN)
        owner = jnp.where(hit, n, owner)
        place = jnp.where(hit, offset, place)
    place = part[:, :128] * OWN + place
    slim = lax.broadcasted_iota(I32, (128, 128), 0)
    face_pick[:, 0:128] = jnp.where(slim == place, 1.0, 0.0).astype(BF16)
    face_pick[:, 128:256] = jnp.where(slim == place + 64, 1.0, 0.0).astype(BF16)
    owner_rows = jnp.broadcast_to(owner, (ROWS, 128))
    right = jnp.zeros((ROWS, 128), F32)
    stab = jnp.zeros((ROWS, 128), F32)

    eight = lax.broadcasted_iota(I32, (8, 128), 0)
    slot_row = lax.broadcasted_iota(I32, (SLOTS, 128), 0).astype(F32)
    wide_slot = jnp.broadcast_to(wanted_f[:, :128], (SLOTS, 128))
    wide_face = jnp.broadcast_to(wanted_f[:, 128:], (SLOTS, 128))
    slot_sum = jnp.zeros((SLOTS, 128), F32)
    face_total = jnp.zeros((SLOTS, 128), F32)
    least = jnp.full((SLOTS, 128), 4096.0, F32)
    for near in (1, 0):
        arrive(0, first, near)
        begin, end = (FAR, KINDS) if near else (0, FAR)
        for base in range(begin, end, 8):
            rows = jnp.zeros((8, 128), F32)
            for n in range(8):
                rows = jnp.where(eight == n, first[base + n, ROWS : ROWS + 8], rows)
            square[base : base + 8] = rows
        held = square[...].T
        for n in range(begin, end):
            column = jnp.broadcast_to(held[0:SLOTS, n : n + 1], (SLOTS, 128))
            code = slot_row + 32.0 * n
            slot_sum = slot_sum + jnp.where(column == wide_slot, code, 0.0)
            if n < SELF and PEERS[n][0] > 0:
                continue
            hit = column == wide_face
            face_total = face_total + jnp.where(hit, code, 0.0)
            least = jnp.minimum(least, jnp.where(hit, code, 4096.0))
        some = [n for n in sources if begin <= n < end]
        sent = jnp.concatenate([first[n, 0:ROWS] for n in some], axis=0)
        high = sent.astype(BF16)
        rest = (sent - high.astype(F32)).astype(BF16)
        found = jnp.dot(high, face_pick[...], preferred_element_type=F32)
        found = found + jnp.dot(rest, face_pick[...], preferred_element_type=F32)
        for at, n in enumerate(some):
            block = found[at * ROWS : (at + 1) * ROWS]
            right = jnp.where(owner_rows == n, block[:, :128], right)
            stab = jnp.where(owner_rows == n, block[:, 128:], stab)
    slot_sum = jnp.sum(slot_sum, axis=0, keepdims=True) - (SELF * 32 + index[:, :128]).astype(F32)
    face_total = jnp.sum(face_total, axis=0, keepdims=True)
    least = jnp.min(least, axis=0, keepdims=True)
    face_code = jnp.where(lane[:, :128] < 64, least, face_total - least)
    code = jnp.concatenate([slot_sum, face_code], axis=1).astype(I32)
    kinds = jnp.where(used, lax.shift_right_arithmetic(code, 5), -1)
    row = jnp.where(used, part * SLOTS + lax.bitwise_and(code, 31), -1)
    deep = lax.broadcasted_iota(I32, (128, 256), 0)
    pick[...] = jnp.where(deep == row, 1.0, 0.0).astype(BF16)
    kind_row[...] = jnp.broadcast_to(kinds, (ROWS, 256))
    scale = 1.0 / jnp.where(owner_rows >= 0, stab, 1.0)
    face_stab = pltpu.roll(first[SELF, 0:ROWS], 64, 1)
    face_scale = 1.0 / jnp.where(small < OWN * PARTS, face_stab, 1.0)

    def gathered(phase, columns, begin, end):
        stack = tiles[phase, begin:end].reshape((end - begin) * ROWS, 128)
        found = jnp.dot(stack, pick[:, columns], preferred_element_type=F32)
        kinds = kind_row[:, columns]
        total = []
        for four in range(begin, end, 4):
            some = jnp.zeros((ROWS, 128), F32)
            for n in range(four, four + 4):
                some = jnp.where(kinds == n, found[(n - begin) * ROWS : (n - begin + 1) * ROWS], some)
            total.append(some)
        while len(total) > 1:
            total = [x + y for x, y in zip(total[::2], total[1::2])]
        return total[0]

    def partners(phase, known):
        arrive(phase + 1, tiles.at[phase], 1)
        known = known + gathered(phase, slice(0, 128), FAR, KINDS)
        arrive(phase + 1, tiles.at[phase], 0)
        return known + gathered(phase, slice(0, 128), 0, FAR)

    def face_sum(phase):
        both = gathered(phase, slice(128, 256), FAR, KINDS) + gathered(phase, slice(128, 256), 0, FAR)
        return both + pltpu.roll(both, 64, 1)

    right = right - partners(0, own)
    rows = to_rows(right * scale)
    for sweep in range(1, SWEEPS):
        own = to_tile(products(rows, schur))
        tiles[sweep, SELF] = own.astype(BF16)
        send(sweep + 1, tiles.at[sweep])
        if sweep == 1:
            face_right = first[SELF, 0:ROWS] - face_sum(0)
        rows = to_rows(partners(sweep, right + own) * scale)

    back = products(rows, couple)
    vol_out[...] = local_rows - jnp.concatenate([back, jnp.zeros((8, 64), F32)], axis=1)
    face_now = (face_right + face_sum(SWEEPS - 1)) * face_scale
    for j in range(PARTS):
        block = pltpu.roll(face_now, 128 - j * OWN, 1) if j else face_now
        square[j * ROWS : (j + 1) * ROWS] = block
    trace_out[...] = square[...].T[0:ROWS]

    leave(0, first)
    for phase in range(SWEEPS):
        leave(phase + 1, tiles.at[phase])


def write(trace_in, vol_in, trace_out, vol_out):
    trace_out[...] = trace_in[0:OWN, 0:80]
    vol_out[...] = vol_in[0:4, 0:320]


def solution(mesh):
    groups, members = mesh.shape["elem"], mesh.shape["face"]
    spec2, spec3 = P(("elem", "face"), None), P(("elem", "face"), None, None)

    def local(vol_inverse, vol_from_trace, trace_from_vol, vol_residual, face_ids, trace_residual, stabilization):
        vmem, hbm = pl.BlockSpec(memory_space=pltpu.VMEM), pl.BlockSpec(memory_space=pl.ANY)
        trace, vol = pl.pallas_call(
            functools.partial(kernel, groups, members),
            out_shape=(pltpu.VMEM((ROWS, 128), F32), pltpu.VMEM((8, 384), F32)),
            in_specs=[hbm] * 7,
            out_specs=(vmem, vmem),
            scratch_shapes=[
                pltpu.SMEM((4, 6), I32),
                pltpu.VMEM((4, 320), BF16),
                pltpu.VMEM((OWN, 80), F32),
                pltpu.VMEM((OWN, 80), F32),
                pltpu.VMEM((4, 320, 320), BF16),
                pltpu.VMEM((4, 320, 480), BF16),
                pltpu.VMEM((4, 320, 480), BF16),
                pltpu.VMEM((4, 512, 320), BF16),
                pltpu.VMEM((4, 512, 512), BF16),
                pltpu.VMEM((KINDS, ROWS + 8, 128), F32),
                pltpu.VMEM((SWEEPS, KINDS, ROWS, 128), BF16),
                pltpu.VMEM((128, 256), BF16),
                pltpu.VMEM((128, 256), BF16),
                pltpu.VMEM((ROWS, 256), I32),
                pltpu.VMEM((128, 128), F32),
                pltpu.SemaphoreType.DMA((7,)),
                pltpu.SemaphoreType.DMA((SWEEPS + 1,)),
                pltpu.SemaphoreType.DMA((SWEEPS + 1, 2)),
            ],
            compiler_params=pltpu.CompilerParams(collective_id=0, has_side_effects=True),
            name="newton",
        )(
            face_ids, vol_inverse, vol_from_trace, jnp.swapaxes(trace_from_vol, 1, 2), vol_residual,
            trace_residual, stabilization,
        )
        return pl.pallas_call(
            write,
            out_shape=(
                jax.ShapeDtypeStruct(trace_residual.shape, F32),
                jax.ShapeDtypeStruct(vol_residual.shape, F32),
            ),
            in_specs=[vmem, vmem],
            out_specs=(vmem, vmem),
            name="write",
        )(pltpu.with_memory_space_constraint(trace, pltpu.VMEM), pltpu.with_memory_space_constraint(vol, pltpu.VMEM))

    return jax.shard_map(
        local,
        mesh=mesh,
        in_specs=(spec3, spec3, spec3, spec2, spec2, spec2, spec2),
        out_specs=(spec2, spec2),
        check_vma=False,
    )
```
